128 devices in a mesh: dp: 8 (over y, core), expert: 16 (over x, z).
Axes of the slice: x: 4, y: 4, z: 4, core: 2. Of those that a mesh axis runs over, the one named last changes fastest.
Arguments:
- tokens: bfloat16 [16384, 2048], P(('dp', 'expert')), may hold values from -6 to 6
- grad_out: bfloat16 [16384, 2048], P(('dp', 'expert')), may hold values from -24 to 24
- routes: int32 [16384, 3], P(('dp', 'expert')), may hold values from 0 to 15, all different within a row; in each aligned block of 128 rows (0 to 127, 128 to 255, ...) at most 32 rows name the same one
- route_weight: bfloat16 [16384, 3], P(('dp', 'expert')), may hold values from 0.099609375 to 1
- w_gate: bfloat16 [16, 2048, 1408], P('expert'), may hold values from -0.125 to 0.125
- w_up: bfloat16 [16, 2048, 1408], P('expert'), may hold values from -0.125 to 0.125
- w_down: bfloat16 [16, 1408, 2048], P('expert'), may hold values from -0.15625 to 0.15625
Outputs:
- token_grad: bfloat16 [16384, 2048], P(('dp', 'expert'))
- prob_grad: bfloat16 [16384, 3], P(('dp', 'expert'))
- wgrad_gate: bfloat16 [16, 2048, 1408], P('expert', 'dp')
- wgrad_up: bfloat16 [16, 2048, 1408], P('expert', 'dp')
- wgrad_down: bfloat16 [16, 1408, 2048], P('expert', None, 'dp')
The draws below stay inside these ranges and needn't reach their ends.
Inputs may be any that keep to these rules, and one draw needn't show every extreme that they name: In each aligned block of 128 tokens (the tokens of one device) no expert is named by more than 32 routes, a bound that some block reaches; the 3 routes of a token name different experts.
All inputs are finite; a program needn't handle non-finite values.
Results may differ from the reference program's by a relative error of at most 0.014.
Values may be sent and summed in bfloat16 or wider, within the bound.
A program may use at most 128 MiB of HBM per device.

```python
import math
import jax
import jax.numpy as jnp
import numpy as np
from jax import lax

D = 2048
FF = 1408
TOP = 3
TOK_DEV = 128
EXPERTS = 16
CAP = 32
TOKENS = 16384
N_DP = 8
N_EXPERT = 16


def strengthened(values, stream_key, source, target, blocks, factor):
    def block_of(dim):
        return (jnp.arange(values.shape[dim]) // (values.shape[dim] // blocks)).reshape((-1,) + (1,) * (values.ndim - 1 - dim))

    first = jax.random.permutation(stream_key, blocks)[block_of(target)]
    other_side = (block_of(target) + blocks // 2) % blocks
    return jnp.where((block_of(source) == first) | (block_of(source) == other_side), factor * values, values)


def level_of(rng, shape, split, smallest, top_value):
    loudness, own = 1.0, jax.random.fold_in(rng, 6)
    for axis_at, shards_of in split:
        heights = jnp.exp(jax.random.uniform(jax.random.fold_in(own, axis_at), (shards_of,), jnp.float32, smallest / len(split), top_value / len(split)))
        loudness = loudness * jnp.repeat(heights, shape[axis_at] // shards_of).reshape([-1 if axis == axis_at else 1 for axis in range(len(shape))])
    return loudness


def deal_out(stream_key, own, number, rows, count, top, limit, slope):
    ranking = jax.random.permutation(stream_key, count)
    crowded, common = portions_of(count, rows * top, limit, slope, True), portions_of(count, rows * top, limit, slope, False)
    places = jnp.arange(count)

    def named(lengths, turn):
        used = int((lengths > 0).sum())
        fixed = max(1, used // 4)
        moved = fixed + (places - fixed + turn * (used - fixed)) % max(1, count - fixed)
        return jnp.zeros((count,), jnp.int32).at[ranking[jnp.where(places < fixed, places, moved)]].set(jnp.asarray(lengths, jnp.int32))

    lengths = jnp.where(number % 4 == 0, named(crowded, number // 4), named(common, number - number // 4 - 1))
    mixed = jax.random.permutation(jax.random.fold_in(own, 3), count)
    giver, sink = mixed[0:count // 2 * 2:2], mixed[1:count // 2 * 2:2]
    room = jnp.minimum(lengths[giver] - 1, limit - lengths[sink]) // 2
    room = jnp.where((giver == ranking[0]) | (sink == ranking[0]) | (lengths[sink] == 0), 0, jnp.maximum(room, 0))
    moved = jax.random.randint(jax.random.fold_in(own, 4), (count // 2,), 0, 1 << 20) % (room + 1)
    lengths = lengths.at[giver].add(-moved).at[sink].add(moved)
    members = jnp.searchsorted(jnp.cumsum(lengths), jnp.arange(rows * top), side="right").astype(jnp.int32)
    table = members.reshape(top, rows).T
    table = table[jax.random.permutation(jax.random.fold_in(own, 1), rows)]
    turn = jax.random.randint(jax.random.fold_in(own, 2), (rows, 1), 0, top)
    return jnp.take_along_axis(table, (jnp.arange(top)[None, :] + turn) % top, axis=1)


def portions_of(count, total, limit, slope, full):
    weights = [(1 << 20) // math.isqrt(standing ** slope) + 1 for standing in range(1, count + 1)]
    largest = limit if full else min(limit, max(-(-total // count), total * weights[0] // sum(weights)))
    least = 1 if total - largest >= count - 1 else 0
    holding, rest = [largest] + [least] * (count - 1), total - largest - least * (count - 1)
    while rest > 0:
        movable = [i for i in range(1, count) if holding[i] < largest] or [i for i in range(1, count) if holding[i] < limit]
        whole, left = sum([weights[i] for i in movable]), rest
        for i in movable:
            extra = min(limit - holding[i], max(1, left * weights[i] // whole), rest)
            holding[i] = holding[i] + extra
            rest = rest - extra
    return np.array(holding)


def gaussian(key, dims, width, most, pieces=(), held_as=jnp.bfloat16):
    result = jax.random.normal(key, dims, jnp.float32) * width
    if len(pieces) > 0:
        result = level_of(key, dims, pieces, -0.22, 0.18) * result
    return jnp.clip(result, min=-most, max=most).astype(held_as)


def gaussian_with(rng, dims, width, most, cuts, heavy, held_as=jnp.bfloat16):
    entries = width * jax.random.normal(rng, dims, jnp.float32)
    if cuts:
        entries = entries * level_of(rng, dims, cuts, -0.22, 0.18)
    return jnp.clip(strengthened(entries, jax.random.fold_in(rng, 3), *heavy), -most, most).astype(held_as)


def setup_inputs(seed: int = 0) -> dict:
    key_list = jax.random.split(jax.random.key(seed), 8)
    tokens = gaussian(key_list[0], (TOKENS, D), 1.0, 6.0, ((0, 128),))
    grad_out = gaussian_with(key_list[1], (TOKENS, D), 1.0, 24.0, ((0, 128),), (0, 1, 128, 5.5))
    routes_keys = jax.random.split(jax.random.fold_in(key_list[2], 1), TOKENS // TOK_DEV)
    routes_turns = jax.random.permutation(jax.random.fold_in(key_list[2], 3), TOKENS // TOK_DEV)
    routes = jax.vmap(lambda own, number: deal_out(jax.random.fold_in(key_list[2], 2), own, number, TOK_DEV, EXPERTS, TOP, CAP, 2))(routes_keys, routes_turns).reshape((TOKENS, TOP))
    route_weight = jnp.clip(jnp.exp(math.log(1.0) - 2.306499 * jax.random.uniform(key_list[3], (TOKENS, TOP), jnp.float32) ** level_of(key_list[3], (TOKENS, TOP), ((0, 128),), -0.2, 0.2)), 0.099609375, 1.0).astype(jnp.bfloat16)
    w_gate = gaussian(key_list[4], (EXPERTS, D, FF), D ** -0.5, 0.125, ((0, 16),))
    w_up = gaussian(key_list[5], (EXPERTS, D, FF), D ** -0.5, 0.125, ((0, 16),))
    w_down = gaussian(key_list[6], (EXPERTS, FF, D), FF ** -0.5, 0.15625, ((0, 16),))
    return dict(tokens=tokens, grad_out=grad_out, routes=routes, route_weight=route_weight, w_gate=w_gate, w_up=w_up, w_down=w_down)


def expert_rows(got_tokens, got_grads, got_weights, gate_mat, up_mat, down_mat):
    pre_gate = jnp.dot(got_tokens, gate_mat, preferred_element_type=jnp.float32)
    pre_up = jnp.dot(got_tokens, up_mat, preferred_element_type=jnp.float32)
    sigma = jax.nn.sigmoid(pre_gate)
    active = pre_gate * sigma
    hidden = (active * pre_up).astype(jnp.bfloat16)
    output = jnp.dot(hidden, down_mat, preferred_element_type=jnp.float32)
    prob_grad = jnp.sum(got_grads.astype(jnp.float32) * output, axis=1).astype(jnp.bfloat16)
    scaled = (got_weights.astype(jnp.float32)[:, None] * got_grads.astype(jnp.float32)).astype(jnp.bfloat16)
    hidden_grad = jnp.dot(scaled, down_mat.T, preferred_element_type=jnp.float32)
    gate_grad = (hidden_grad * pre_up * sigma * (1.0 + pre_gate * (1.0 - sigma))).astype(jnp.bfloat16)
    up_grad = (hidden_grad * active).astype(jnp.bfloat16)
    input_grad = jnp.dot(gate_grad, gate_mat.T, preferred_element_type=jnp.float32)
    input_grad = (input_grad + jnp.dot(up_grad, up_mat.T, preferred_element_type=jnp.float32)).astype(jnp.bfloat16)
    return input_grad, prob_grad, hidden, scaled, gate_grad, up_grad


def rounded_sum(partials):
    kept = lax.optimization_barrier(partials.astype(jnp.bfloat16))
    return jnp.sum(kept.astype(jnp.float32), axis=0).astype(jnp.bfloat16)


def reference(tokens, grad_out, routes, route_weight, w_gate, w_up, w_down):
    devices = N_DP * N_EXPERT
    flat_ids = routes.reshape(devices, TOK_DEV * TOP)
    onehot = (flat_ids[:, :, None] == jnp.arange(EXPERTS, dtype=jnp.int32)[None, None, :]).astype(jnp.int32)
    before = jnp.cumsum(onehot, axis=1) - onehot
    slot_pos = jnp.sum(before * onehot, axis=2).astype(jnp.int32)
    column = (jnp.arange(devices, dtype=jnp.int32)[:, None] * CAP + slot_pos).reshape(-1)
    expert = flat_ids.reshape(-1)
    slot_span = devices * CAP
    token_rep = jnp.repeat(tokens, TOP, axis=0)
    grad_rep = jnp.repeat(grad_out, TOP, axis=0)
    buf_tokens = jnp.zeros((EXPERTS, slot_span, D), jnp.bfloat16).at[expert, column].set(token_rep)
    buf_grads = jnp.zeros((EXPERTS, slot_span, D), jnp.bfloat16).at[expert, column].set(grad_rep)
    buf_weights = jnp.zeros((EXPERTS, slot_span), jnp.bfloat16).at[expert, column].set(route_weight.reshape(-1))
    row_group = N_EXPERT * CAP

    def one_expert(bundle):
        got_tokens, got_grads, got_weights, gate_mat, up_mat, down_mat = bundle
        input_grad, prob_grad, hidden, scaled, gate_grad, up_grad = expert_rows(
            got_tokens, got_grads, got_weights, gate_mat, up_mat, down_mat)
        token_blocks = got_tokens.reshape(N_DP, row_group, D).astype(jnp.float32)
        scaled_blocks = scaled.reshape(N_DP, row_group, D).astype(jnp.float32)
        hidden_blocks = hidden.reshape(N_DP, row_group, FF).astype(jnp.float32)
        part_gate = jnp.einsum("nsd,nsf->ndf", token_blocks, gate_grad.reshape(N_DP, row_group, FF).astype(jnp.float32))
        part_up = jnp.einsum("nsd,nsf->ndf", token_blocks, up_grad.reshape(N_DP, row_group, FF).astype(jnp.float32))
        part_down = jnp.einsum("nsf,nsd->nfd", hidden_blocks, scaled_blocks)
        return input_grad, prob_grad, rounded_sum(part_gate), rounded_sum(part_up), rounded_sum(part_down)

    results = lax.map(one_expert, (buf_tokens, buf_grads, buf_weights, w_gate, w_up, w_down))
    route_grad = results[0][expert, column]
    token_grad = jnp.sum(route_grad.reshape(TOKENS, TOP, D).astype(jnp.float32), axis=1).astype(jnp.bfloat16)
    prob_grad = results[1][expert, column].reshape(TOKENS, TOP)
    return token_grad, prob_grad, results[2], results[3], results[4]
```

```python
import jax
import jax.numpy as jnp
from jax import lax
from jax.sharding import PartitionSpec as P


def slot_onehots(routes, experts, capacity):
    tok_rows, route_count = routes.shape
    flat_ids = routes.reshape(-1)
    onehot = (flat_ids[:, None] == jnp.arange(experts, dtype=jnp.int32)[None, :]).astype(jnp.int32)
    before = jnp.cumsum(onehot, axis=0) - onehot
    slot_pos = jnp.sum(before * onehot, axis=1)
    places = flat_ids * capacity + slot_pos
    slots = jnp.arange(experts * capacity, dtype=jnp.int32)
    route_hot = (places[None, :] == slots[:, None]).astype(jnp.bfloat16)
    token_hot = jnp.sum(
        route_hot.reshape(experts * capacity, tok_rows, route_count).astype(jnp.float32), axis=2
    ).astype(jnp.bfloat16)
    return route_hot, token_hot


def right_product(left, right):
    return lax.dot_general(
        left, right, (((1,), (1,)), ((), ())), preferred_element_type=jnp.float32
    )


def left_product(left, right):
    return lax.dot_general(
        left, right, (((0,), (0,)), ((), ())), preferred_element_type=jnp.float32
    )


def plain_product(left, right):
    return jnp.dot(left, right, preferred_element_type=jnp.float32)


def expert_a2a(x):
    experts = lax.axis_size("expert")
    shape = x.shape
    out = lax.all_to_all(
        x.reshape((experts, shape[0] // experts) + shape[1:]), "expert",
        split_axis=0, concat_axis=0, tiled=True,
    )
    return out.reshape(shape)


def body(tokens, grad_out, routes, route_weight, w_gate, w_up, w_down):
    tok_rows, model_width = tokens.shape
    route_count = routes.shape[1]
    experts = lax.axis_size("expert")
    capacity = 4 * tok_rows * route_count // (3 * experts)
    route_hot, token_hot = slot_onehots(routes, experts, capacity)
    send_tokens = plain_product(token_hot, tokens).astype(jnp.bfloat16)
    send_grads = plain_product(token_hot, grad_out).astype(jnp.bfloat16)
    send_weights = plain_product(route_hot, route_weight.reshape(-1, 1)).astype(jnp.bfloat16)
    got_tokens = expert_a2a(send_tokens)
    got_grads = expert_a2a(send_grads)
    got_weights = expert_a2a(send_weights)[:, 0]

    gate_mat = w_gate[0]
    up_mat = w_up[0]
    down_mat = w_down[0]
    pre_gate = plain_product(got_tokens, gate_mat)
    pre_up = plain_product(got_tokens, up_mat)
    sigma = jax.nn.sigmoid(pre_gate)
    active = pre_gate * sigma
    hidden = (active * pre_up).astype(jnp.bfloat16)
    scaled = (got_weights.astype(jnp.float32)[:, None] * got_grads.astype(jnp.float32)).astype(
        jnp.bfloat16
    )
    part_down = left_product(scaled, hidden).astype(jnp.bfloat16)
    sum_down = lax.psum_scatter(part_down, "dp", scatter_dimension=0, tiled=True)
    output = plain_product(hidden, down_mat)
    prob_grad = jnp.sum(got_grads.astype(jnp.float32) * output, axis=1).astype(jnp.bfloat16)
    hidden_grad = right_product(scaled, down_mat)
    gate_grad = (hidden_grad * pre_up * sigma * (1.0 + pre_gate * (1.0 - sigma))).astype(
        jnp.bfloat16
    )
    up_grad = (hidden_grad * active).astype(jnp.bfloat16)
    part_gate = left_product(got_tokens, gate_grad).astype(jnp.bfloat16)
    sum_gate = lax.psum_scatter(part_gate, "dp", scatter_dimension=0, tiled=True)
    part_up = left_product(got_tokens, up_grad).astype(jnp.bfloat16)
    sum_up = lax.psum_scatter(part_up, "dp", scatter_dimension=0, tiled=True)
    input_grad = (right_product(gate_grad, gate_mat) + right_product(up_grad, up_mat)).astype(
        jnp.bfloat16
    )
    back_grads = expert_a2a(input_grad)
    back_probs = expert_a2a(prob_grad.reshape(-1, 1))
    token_grad = left_product(token_hot, back_grads).astype(jnp.bfloat16)
    prob_out = left_product(route_hot, back_probs).astype(jnp.bfloat16).reshape(tok_rows, route_count)
    wgrad_gate = sum_gate[None]
    wgrad_up = sum_up[None]
    wgrad_down = sum_down.T[None]
    return (token_grad, prob_out, wgrad_gate, wgrad_up, wgrad_down)


def solution(mesh):
    in_specs = (
        P(("dp", "expert"), None),
        P(("dp", "expert"), None),
        P(("dp", "expert"), None),
        P(("dp", "expert"), None),
        P("expert", None, None),
        P("expert", None, None),
        P("expert", None, None),
    )
    out_specs = (
        P(("dp", "expert"), None),
        P(("dp", "expert"), None),
        P("expert", "dp", None),
        P("expert", "dp", None),
        P("expert", None, "dp"),
    )
    return jax.shard_map(body, mesh=mesh, in_specs=in_specs, out_specs=out_specs, check_vma=False)
```
